32 devices in a mesh: row: 4 (over x, core), col: 8 (over z, y).
Axes of the slice: x: 2, y: 2, z: 4, core: 2. Of those that a mesh axis runs over, the one named last changes fastest.
Arguments:
- rhs: float32 [4, 8, 8192], P(None, None, 'row'), may hold values from -6 to 6
- off_blocks: float32 [6, 8192, 8192], P(None, 'row', 'col'), may hold values from -0.046875 to 0.046875
- inverse_blocks: float32 [4, 8192, 8192], P(None, 'row', 'col'), as said below
- pivots: float32 [4, 8192], replicated, may hold values from 0.5 to 2
Outputs:
- solution: float32 [4, 8, 8192], P(None, None, 'col')
The draws below stay inside these ranges and needn't reach their ends.
Inputs may be any that keep to these rules, and one draw needn't show every extreme that they name: `inverse_blocks`: each block is unit lower triangular: ones on the diagonal, zeros above it.
All inputs are finite; a program needn't handle non-finite values.
Results may differ from the reference program's by a relative error of at most 0.00013.
Values sent between devices are 32-bit elements; how exact they have to be, the bound alone decides.
A program may use at most 128 MiB of HBM per device.

```python
import math
import jax
import jax.numpy as jnp
from jax import lax

PW = 8192
PANELS = 4
NRHS = 8
NB = 6


def draw_inverse_blocks(key, part):
    noise = jax.random.normal(key, (PANELS, PW, PW), jnp.float32)
    lower = jnp.tril(noise, -1) * PW ** (-0.5)
    return lower + jnp.eye(PW, dtype=jnp.float32)[None, :, :]


def level_of(own_key, dims, split, least, largest):
    def one(axis_at, parts):
        steps = jax.random.uniform(jax.random.fold_in(jax.random.fold_in(own_key, 6), axis_at), (parts,), jnp.float32, least / len(split), largest / len(split))
        return jnp.repeat(jnp.exp(steps), dims[axis_at] // parts).reshape((-1,) + (1,) * (len(dims) - axis_at - 1))

    level = one(*split[0])
    for cut in split[1:]:
        level = level * one(*cut)
    return level


def normal_values(key, extent, width, bound, shards=(), kind=jnp.bfloat16):
    drawn = jax.random.normal(key, extent, jnp.float32) * width
    if len(shards) > 0:
        drawn = level_of(key, extent, shards, -0.22, 0.18) * drawn
    return jnp.clip(drawn, min=-bound, max=bound).astype(kind)


def setup_inputs(seed: int = 0) -> dict:
    seeds = jax.random.split(jax.random.key(seed), 5)
    rhs = normal_values(seeds[0], (PANELS, NRHS, PW), 1.0, 6.0, ((2, 4),), jnp.float32)
    off_blocks = normal_values(seeds[1], (NB, PW, PW), (2 * PW) ** -0.5, 0.046875, ((1, 4), (2, 8)), jnp.float32)
    inverse_blocks = draw_inverse_blocks(jax.random.fold_in(seeds[4], 71), 0)
    pivots = jnp.clip(jnp.exp(jax.random.uniform(seeds[3], (PANELS, PW), jnp.float32, math.log(0.5), math.log(2.0))), 0.5, 2.0)
    return {"rhs": rhs, "off_blocks": off_blocks, "inverse_blocks": inverse_blocks, "pivots": pivots}


def block_slot(target, source):
    return source * PANELS - source * (source + 1) // 2 + (target - source - 1)


def times_transposed(left, right):
    return jnp.dot(left, right.T, precision=lax.Precision.HIGHEST, preferred_element_type=jnp.float32)


def times_plain(left, right):
    return jnp.dot(left, right, precision=lax.Precision.HIGHEST, preferred_element_type=jnp.float32)


def reference(rhs, off_blocks, inverse_blocks, pivots):
    solved = []
    for target in range(PANELS):
        current = rhs[target]
        for source in range(target):
            current = current - times_transposed(solved[source], off_blocks[block_slot(target, source)])
        solved.append(times_transposed(current, inverse_blocks[target]))
    results = [None] * PANELS
    for target in reversed(range(PANELS)):
        scaled = solved[target] / pivots[target][None, :]
        for later in range(target + 1, PANELS):
            scaled = scaled - times_plain(results[later], off_blocks[block_slot(later, target)])
        results[target] = times_plain(scaled, inverse_blocks[target])
    return jnp.stack(results)
```

```python
import functools

import jax
import jax.numpy as jnp
from jax import lax
from jax.experimental import pallas as pl
from jax.experimental.pallas import tpu as pltpu
from jax.sharding import PartitionSpec as P

MESH = pl.DeviceIdType.MESH


def block_slot(target, source, count):
    return source * count - source * (source + 1) // 2 + (target - source - 1)


def split_rows(value):
    high = value.astype(jnp.bfloat16)
    low = (value - high.astype(jnp.float32)).astype(jnp.bfloat16)
    return high, low


def stacked(value):
    high = value.astype(jnp.bfloat16).astype(jnp.float32)
    return jnp.concatenate([high, value - high], axis=0).astype(jnp.bfloat16)


def kernel(R, C, rhs_ref, piv_ref, off_ref, inv_ref, out_ref,
           wbuf, pend, bpend, wb, send1, recv1, gat, senda, recva, rowb, xg, xs, xr,
           load_sem, s1s, s1r, s2s, s2r, sas, sar, sbs, sbr, sxs, sxr, sfs, sfr):
    count = inv_ref.shape[0]
    W = inv_ref.shape[2]
    ratio = C // R
    nred, CH = gat.shape[1], gat.shape[3]
    NT = ratio * nred
    r = lax.axis_index("row")
    c = lax.axis_index("col")
    home = c // ratio
    part = c % ratio
    diag = r == home

    def source(name):
        kind, i, k = name
        if kind == "m":
            return inv_ref.at[k]
        return off_ref.at[block_slot(i, k, count)]

    where = {}
    load_id = [0]
    waiting = {}

    def load(name, slot):
        copy = pltpu.make_async_copy(source(name), wbuf.at[slot], load_sem.at[load_id[0]])
        load_id[0] += 1
        copy.start()
        for old in [n for n, s in where.items() if s == slot]:
            del where[old]
        where[name] = slot
        waiting[name] = copy

    def ready(name):
        if name in waiting:
            waiting.pop(name).wait()
        return where[name]

    M = lambda k: ("m", k, k)
    L = lambda i, k: ("l", i, k)
    slots = wbuf.shape[0]

    uses = []
    late = []
    for k in range(count):
        uses.append(M(k))
        if late:
            uses.append(late.pop(0))
        if k + 1 < count:
            uses.append(L(k + 1, k))
        late = late + [L(i, k) for i in range(k + 2, count)]
        late.sort(key=lambda n: n[1])
        if late:
            uses.append(late.pop(0))
    blate = []
    for k in reversed(range(count)):
        uses.append(M(k))
        if blate:
            uses.append(blate.pop(0))
        if k > 0:
            uses.append(L(k, k - 1))
        blate = blate + [L(k, j) for j in reversed(range(k - 1))]
        blate.sort(key=lambda n: -n[2])
        if blate:
            uses.append(blate.pop(0))
    position = [0]

    def prefetch(most):
        now = position[0]
        started = 0
        for at in range(now, len(uses)):
            name = uses[at]
            if name in where:
                continue
            free = [s for s in range(slots) if s not in where.values()]
            if free:
                slot = free[0]
            else:
                def next_use(n):
                    later = [u for u in range(now, len(uses)) if uses[u] == n]
                    return later[0] if later else len(uses) + 1
                victim = max(where, key=next_use)
                if next_use(victim) <= at or victim in waiting:
                    return
                slot = where[victim]
            load(name, slot)
            started += 1
            if started == most:
                return

    def used(name):
        assert uses[position[0]] == name
        position[0] += 1

    prefetch(3)

    barrier = pltpu.get_barrier_semaphore()

    def greet(row, col):
        @pl.when(jnp.logical_not(jnp.logical_and(row == r, col == c)))
        def _():
            pl.semaphore_signal(barrier, inc=1, device_id=(row, col), device_id_type=MESH)

    for h in range(ratio):
        for q in range(R):
            greet(jnp.int32(q), r * ratio + h)
    for cc in range(C):
        greet(home, jnp.int32(cc))
    for d in range(1, R):
        pl.semaphore_signal(barrier, inc=1, device_id=(lax.rem(r + d, R), c), device_id_type=MESH)
    pl.semaphore_wait(barrier, ratio * R + C + R - 1 - 2 * diag.astype(jnp.int32))

    def remote(src, dst, ssem, rsem, row, col):
        return pltpu.make_async_remote_copy(
            src_ref=src, dst_ref=dst, send_sem=ssem, recv_sem=rsem,
            device_id=(row, col), device_id_type=MESH)

    def take(ref, sem):
        pltpu.make_async_copy(ref, ref, sem).wait()

    def reducers(body):
        if nred == R:
            body()
        else:
            pl.when(r < nred)(body)

    ends = []

    def send_or_keep(src, dst, ssem, rsem, row, col):
        same = jnp.logical_and(row == r, col == c)

        @pl.when(same)
        def _():
            pltpu.make_async_copy(src, dst, rsem).start()

        @pl.when(jnp.logical_not(same))
        def _():
            remote(src, dst, ssem, rsem, row, col).start()

    def scatter_rows(s):
        for h in range(ratio):
            for q in range(nred):
                send_or_keep(send1.at[s, h * nred + q], recv1.at[s, c], s1s.at[s], s1r.at[s],
                             jnp.int32(q), r * ratio + h)

        def end():
            kept = jnp.logical_and(diag, r < nred)

            @pl.when(kept)
            def _():
                take(send1.at[s, pl.ds(0, NT - 1)], s1s.at[s])

            @pl.when(jnp.logical_not(kept))
            def _():
                take(send1.at[s], s1s.at[s])
        ends.append(end)

    def sum_rows(s, entry):
        def body():
            take(recv1.at[s], s1r.at[s])
            gat[entry, r] = jnp.sum(recv1[s], axis=0)
        reducers(body)

    def gather_start(buf, ssem, rsem):
        def body():
            for d in range(1, R):
                remote(buf.at[r], buf.at[r], ssem, rsem, lax.rem(r + d, R), c).start()
        reducers(body)

        def end():
            def body():
                for_all = recva.at[0, pl.ds(0, R - 1)]
                take(for_all, ssem)
            reducers(body)
        ends.append(end)

    def gather_wait(buf, rsem):
        if nred == R:
            take(buf.at[pl.ds(0, nred - 1)], rsem)
        else:
            @pl.when(r < nred)
            def _():
                take(buf.at[pl.ds(0, nred - 1)], rsem)

            @pl.when(r >= nred)
            def _():
                take(buf, rsem)

    def scatter_cols(s):
        for d in range(1, R):
            q = lax.rem(r + d, R)

            def body(q=q):
                remote(senda.at[s, q], recva.at[s, r], sas.at[s], sar.at[s], q, c).start()
            if nred == R:
                body()
            else:
                pl.when(q < nred)(body)

        def keep():
            recva[s, r] = senda[s, r]
        reducers(keep)

        def end():
            gather_wait(senda.at[s], sas.at[s])
        ends.append(end)

    def sum_cols(s):
        take(recva.at[s, pl.ds(0, R - 1)], sar.at[s])
        return jnp.sum(recva[s], axis=0)

    def spread_rows(s, src):
        def body():
            slot = part * nred + r
            for cc in range(C):
                send_or_keep(src, rowb.at[s, slot], sbs.at[s], sbr.at[s], home, jnp.int32(cc))
        reducers(body)

        def end():
            def body():
                @pl.when(diag)
                def _():
                    take(recv1.at[0, pl.ds(0, C - 1)], sbs.at[s])

                @pl.when(jnp.logical_not(diag))
                def _():
                    take(recv1.at[0], sbs.at[s])
            reducers(body)
        ends.append(end)

    def spread_wait(s):
        take(rowb.at[s], sbr.at[s])

    def times_rows(name, s, emit):
        slot = ready(name)
        left = stacked(jnp.concatenate([gat[s, q] for q in range(nred)], axis=1))

        def step(t, _):
            high, low = split_rows(wbuf[slot, pl.ds(pl.multiple_of(t * CH, CH), CH), :])
            dims = (((1,), (1,)), ((), ()))
            both = lax.dot_general(left, high, dims, preferred_element_type=jnp.float32)
            both += lax.dot_general(left, low, dims, preferred_element_type=jnp.float32)
            n = both.shape[0] // 2
            emit(t, both[:n] + both[n:])
            return 0

        lax.fori_loop(0, NT, step, 0)
        used(name)

    def times_cols(name, s):
        slot = ready(name)
        n = rowb.shape[2]

        def step(t, total):
            left = stacked(rowb[s, t])
            high, low = split_rows(wbuf[slot, pl.ds(pl.multiple_of(t * CH, CH), CH), :])
            total += jnp.dot(left, high, preferred_element_type=jnp.float32)
            return total + jnp.dot(left, low, preferred_element_type=jnp.float32)

        total = lax.fori_loop(0, NT, step, jnp.zeros((2 * n, W), jnp.float32))
        used(name)
        return total[:n] + total[n:]

    @pl.when(diag)
    def _():
        for q in range(nred):
            gat[0, q] = rhs_ref[0, :, pl.ds(pl.multiple_of(part * W + q * CH, CH), CH)]
        for d in range(1, R):
            remote(gat.at[0], gat.at[0], s2s.at[0], s2r.at[0], lax.rem(r + d, R), c).start()

    def end_first():
        @pl.when(diag)
        def _():
            take(xr.at[pl.ds(0, R - 1)], s2s.at[0])
    ends.append(end_first)
    own = c == r * ratio
    for k in range(1, count):
        for t in range(NT):
            pend[k, t] = jnp.where(own, rhs_ref[k, :, t * CH:(t + 1) * CH], 0.0)

    @pl.when(jnp.logical_not(diag))
    def _():
        take(gat.at[0], s2r.at[0])

    late = []

    def fill_late():
        if late:
            i, k, s = late.pop(0)

            def emit(t, value, i=i):
                pend[i, t] = pend[i, t] - value
            times_rows(L(i, k), s, emit)

    col_at = 0
    stage = 0
    for k in range(count):
        def emit(t, value, s=stage):
            send1[s, t] = value
        times_rows(M(k), col_at, emit)
        scatter_rows(stage)
        prefetch(2)
        fill_late()
        entry = stage + 1
        sum_rows(stage, entry)
        stage += 1
        if k == count - 1:
            break
        gather_start(gat.at[entry], s2s.at[entry], s2r.at[entry])
        gather_wait(gat.at[entry], s2r.at[entry])
        late = late + [(i, k, entry) for i in range(k + 2, count)]

        def emit_l(t, value, s=stage, i=k + 1):
            send1[s, t] = pend[i, t] - value
        times_rows(L(k + 1, k), entry, emit_l)
        scatter_rows(stage)
        prefetch(2)
        late.sort(key=lambda n: n[0])
        fill_late()
        entry = stage + 1
        sum_rows(stage, entry)
        gather_start(gat.at[entry], s2s.at[entry], s2r.at[entry])
        gather_wait(gat.at[entry], s2r.at[entry])
        col_at = entry
        stage += 1

    def pivot(k):
        return piv_ref[k:k + 1, pl.ds(pl.multiple_of(c * W + r * CH, CH), CH)]

    n_cols = 0
    n_rows = 0

    def scale_last():
        wb[count - 1] = gat[2 * count - 1, r] / pivot(count - 1)
    reducers(scale_last)
    spread_rows(0, wb.at[count - 1])
    n_rows = 1
    blate = []

    def fill_blate():
        if blate:
            i, j, s = blate.pop(0)
            total = times_cols(L(i, j), s)
            if i == count - 1:
                bpend[j] = total
            else:
                bpend[j] = bpend[j] + total

    def put_cols(total, s):
        for q in range(nred):
            senda[s, q] = total[:, q * CH:(q + 1) * CH]

    for k in reversed(range(count)):
        prefetch(2)
        fill_blate()
        spread_wait(n_rows - 1)
        total = times_cols(M(k), n_rows - 1)
        if k == 0:
            for q in range(nred):
                xs[q] = total[:, q * CH:(q + 1) * CH]
            for d in range(1, R):
                remote(xs, xr.at[r], sfs.at[0], sfr.at[0], lax.rem(r + d, R), c).start()
            xr[r] = xs[...]
            break
        put_cols(total, n_cols)
        scatter_cols(n_cols)
        prefetch(2)

        def keep_answer(k=k, s=n_cols):
            xg[k, r] = sum_cols(s)
        reducers(keep_answer)
        n_cols += 1
        spread_rows(n_rows, xg.at[k, r])
        n_rows += 1
        gather_start(xg.at[k], sxs.at[k], sxr.at[k])
        fill_blate()
        spread_wait(n_rows - 1)
        total = times_cols(L(k, k - 1), n_rows - 1)
        if k < count - 1:
            total = bpend[k - 1] + total
        put_cols(total, n_cols)
        scatter_cols(n_cols)
        prefetch(2)

        def scale(k=k, s=n_cols):
            wb[k - 1] = gat[2 * k - 1, r] / pivot(k - 1) - sum_cols(s)
        reducers(scale)
        n_cols += 1
        spread_rows(n_rows, wb.at[k - 1])
        n_rows += 1
        blate = blate + [(k, j, n_rows - 2) for j in reversed(range(k - 1))]
        blate.sort(key=lambda n: -n[1])

    for k in range(1, count):
        gather_wait(xg.at[k], sxr.at[k])
        for q in range(nred):
            out_ref[k, :, q * CH:(q + 1) * CH] = xg[k, q]
    for end in ends:
        end()
    take(xr.at[pl.ds(0, R - 1)], sfr.at[0])
    summed = jnp.sum(xr[...], axis=0)
    for q in range(nred):
        out_ref[0, :, q * CH:(q + 1) * CH] = summed[q]
    take(xr.at[pl.ds(0, R - 1)], sfs.at[0])
    assert position[0] == len(uses)


def local(R, C, rhs, off_blocks, inverse_blocks, pivots):
    count, rows_tile, W = inverse_blocks.shape
    n = rhs.shape[1]
    nred = max(1, min(R, W // 128))
    CH = W // nred
    NT = rows_tile // CH
    f32 = jnp.float32
    blocks = count + off_blocks.shape[0]
    slots = min(blocks, (56 << 20) // (rows_tile * W * 4))
    dma = pltpu.SemaphoreType.DMA
    vmem = pl.BlockSpec(memory_space=pltpu.VMEM)
    hbm = pl.BlockSpec(memory_space=pl.ANY)
    return pl.pallas_call(
        functools.partial(kernel, R, C),
        out_shape=jax.ShapeDtypeStruct((count, n, W), f32),
        in_specs=[vmem, vmem, hbm, hbm],
        out_specs=vmem,
        scratch_shapes=[
            pltpu.VMEM((slots, rows_tile, W), f32),
            pltpu.VMEM((count, NT, n, CH), f32),
            pltpu.VMEM((count, n, W), f32),
            pltpu.VMEM((count, n, CH), f32),
            pltpu.VMEM((2 * count - 1, NT, n, CH), f32),
            pltpu.VMEM((2 * count - 1, C, n, CH), f32),
            pltpu.VMEM((2 * count, nred, n, CH), f32),
            pltpu.VMEM((2 * count - 2, nred, n, CH), f32),
            pltpu.VMEM((2 * count - 2, R, n, CH), f32),
            pltpu.VMEM((2 * count - 1, NT, n, CH), f32),
            pltpu.VMEM((count, nred, n, CH), f32),
            pltpu.VMEM((nred, n, CH), f32),
            pltpu.VMEM((R, nred, n, CH), f32),
            dma((2 * blocks,)),
            dma((2 * count - 1,)), dma((2 * count - 1,)),
            dma((2 * count,)), dma((2 * count,)),
            dma((2 * count - 2,)), dma((2 * count - 2,)),
            dma((2 * count - 1,)), dma((2 * count - 1,)),
            dma((count,)), dma((count,)),
            dma((1,)), dma((1,)),
        ],
        compiler_params=pltpu.CompilerParams(
            collective_id=0, has_side_effects=True, vmem_limit_bytes=67043328),
    )(rhs, pivots, off_blocks, inverse_blocks)


def solution(mesh):
    return jax.shard_map(
        functools.partial(local, mesh.shape["row"], mesh.shape["col"]),
        mesh=mesh,
        in_specs=(P(None, None, "row"), P(None, "row", "col"), P(None, "row", "col"), P()),
        out_specs=P(None, None, "col"),
        check_vma=False,
    )
```

```python
import functools

import jax
import jax.numpy as jnp
from jax import lax
from jax.experimental import pallas as pl
from jax.experimental.pallas import tpu as pltpu
from jax.sharding import PartitionSpec as P

MESH = pl.DeviceIdType.MESH


def block_slot(target, source, count):
    return source * count - source * (source + 1) // 2 + (target - source - 1)


def split_rows(value):
    high = value.astype(jnp.bfloat16)
    low = (value - high.astype(jnp.float32)).astype(jnp.bfloat16)
    return high, low


def stacked(value):
    high = value.astype(jnp.bfloat16).astype(jnp.float32)
    return jnp.concatenate([high, value - high], axis=0).astype(jnp.bfloat16)


def kernel(R, C, rhs_ref, piv_ref, off_ref, inv_ref, out_ref,
           wbuf, pend, bpend, wb, send1, recv1, gat, senda, recva, rowb, xg, xs, xr,
           load_sem, s1s, s1r, s2s, s2r, sas, sar, sbs, sbr, sxs, sxr, sfs, sfr):
    count = inv_ref.shape[0]
    W = inv_ref.shape[2]
    ratio = C // R
    nred, CH = gat.shape[1], gat.shape[3]
    NT = ratio * nred
    r = lax.axis_index("row")
    c = lax.axis_index("col")
    home = c // ratio
    part = c % ratio
    diag = r == home

    def source(name):
        kind, i, k = name
        if kind == "m":
            return inv_ref.at[k]
        return off_ref.at[block_slot(i, k, count)]

    where = {}
    load_id = [0]
    waiting = {}

    def load(name, slot):
        copy = pltpu.make_async_copy(source(name), wbuf.at[slot], load_sem.at[load_id[0]])
        load_id[0] += 1
        copy.start()
        for old in [n for n, s in where.items() if s == slot]:
            del where[old]
        where[name] = slot
        waiting[name] = copy

    def ready(name):
        if name in waiting:
            waiting.pop(name).wait()
        return where[name]

    M = lambda k: ("m", k, k)
    L = lambda i, k: ("l", i, k)
    slots = wbuf.shape[0]

    uses = []
    late = []
    for k in range(count):
        uses.append(M(k))
        if late:
            uses.append(late.pop(0))
        if k + 1 < count:
            uses.append(L(k + 1, k))
        late = late + [L(i, k) for i in range(k + 2, count)]
        late.sort(key=lambda n: n[1])
        if late:
            uses.append(late.pop(0))
    blate = []
    for k in reversed(range(count)):
        uses.append(M(k))
        if blate:
            uses.append(blate.pop(0))
        if k > 0:
            uses.append(L(k, k - 1))
        blate = blate + [L(k, j) for j in reversed(range(k - 1))]
        blate.sort(key=lambda n: -n[2])
        if blate:
            uses.append(blate.pop(0))
    position = [0]

    def prefetch(most):
        now = position[0]
        started = 0
        for at in range(now, len(uses)):
            name = uses[at]
            if name in where:
                continue
            free = [s for s in range(slots) if s not in where.values()]
            if free:
                slot = free[0]
            else:
                def next_use(n):
                    later = [u for u in range(now, len(uses)) if uses[u] == n]
                    return later[0] if later else len(uses) + 1
                victim = max(where, key=next_use)
                if next_use(victim) <= at or victim in waiting:
                    return
                slot = where[victim]
            load(name, slot)
            started += 1
            if started == most:
                return

    def used(name):
        assert uses[position[0]] == name
        position[0] += 1

    prefetch(3)

    barrier = pltpu.get_barrier_semaphore()

    def greet(row, col):
        @pl.when(jnp.logical_not(jnp.logical_and(row == r, col == c)))
        def _():
            pl.semaphore_signal(barrier, inc=1, device_id=(row, col), device_id_type=MESH)

    for h in range(ratio):
        for q in range(R):
            greet(jnp.int32(q), r * ratio + h)
    for cc in range(C):
        greet(home, jnp.int32(cc))
    for d in range(1, R):
        pl.semaphore_signal(barrier, inc=1, device_id=(lax.rem(r + d, R), c), device_id_type=MESH)
    pl.semaphore_wait(barrier, ratio * R + C + R - 1 - 2 * diag.astype(jnp.int32))

    def remote(src, dst, ssem, rsem, row, col):
        return pltpu.make_async_remote_copy(
            src_ref=src, dst_ref=dst, send_sem=ssem, recv_sem=rsem,
            device_id=(row, col), device_id_type=MESH)

    def take(ref, sem):
        pltpu.make_async_copy(ref, ref, sem).wait()

    def reducers(body):
        if nred == R:
            body()
        else:
            pl.when(r < nred)(body)

    ends = []

    def send_or_keep(src, dst, ssem, rsem, row, col):
        same = jnp.logical_and(row == r, col == c)

        @pl.when(same)
        def _():
            pltpu.make_async_copy(src, dst, rsem).start()

        @pl.when(jnp.logical_not(same))
        def _():
            remote(src, dst, ssem, rsem, row, col).start()

    def far_first(j):
        at = lax.rem(j, nred)
        q = at
        if nred % 2 == 0:
            chip = lax.rem(r // 2 + 1 + at // 2, nred // 2)
            q = chip * 2 + lax.rem(r + 1 + at, 2)
        return lax.rem(part + 1 + j // nred, ratio) * nred + q

    def scatter_tile(s, t):
        send_or_keep(send1.at[s, t], recv1.at[s, c], s1s.at[s], s1r.at[s],
                     lax.rem(t, nred), r * ratio + t // nred)

    def scatter_rows_ends(s):
        def end():
            kept = jnp.logical_and(diag, r < nred)

            @pl.when(kept)
            def _():
                take(send1.at[s, pl.ds(0, NT - 1)], s1s.at[s])

            @pl.when(jnp.logical_not(kept))
            def _():
                take(send1.at[s], s1s.at[s])
        ends.append(end)

    def sum_rows(s, entry):
        def body():
            take(recv1.at[s], s1r.at[s])
            gat[entry, r] = jnp.sum(recv1[s], axis=0)
        reducers(body)

    def gather_start(buf, ssem, rsem):
        def body():
            for d in range(1, R):
                remote(buf.at[r], buf.at[r], ssem, rsem, lax.rem(r + d, R), c).start()
        reducers(body)

        def end():
            def body():
                for_all = recva.at[0, pl.ds(0, R - 1)]
                take(for_all, ssem)
            reducers(body)
        ends.append(end)

    def gather_wait(buf, rsem):
        if nred == R:
            take(buf.at[pl.ds(0, nred - 1)], rsem)
        else:
            @pl.when(r < nred)
            def _():
                take(buf.at[pl.ds(0, nred - 1)], rsem)

            @pl.when(r >= nred)
            def _():
                take(buf, rsem)

    def scatter_cols(s):
        for d in range(1, R):
            q = lax.rem(r + d, R)

            def body(q=q):
                remote(senda.at[s, q], recva.at[s, r], sas.at[s], sar.at[s], q, c).start()
            if nred == R:
                body()
            else:
                pl.when(q < nred)(body)

        def keep():
            recva[s, r] = senda[s, r]
        reducers(keep)

        def end():
            gather_wait(senda.at[s], sas.at[s])
        ends.append(end)

    def sum_cols(s):
        take(recva.at[s, pl.ds(0, R - 1)], sar.at[s])
        return jnp.sum(recva[s], axis=0)

    def spread_rows(s, src):
        def body():
            slot = part * nred + r
            for cc in range(C):
                send_or_keep(src, rowb.at[s, slot], sbs.at[s], sbr.at[s, slot], home, jnp.int32(cc))
        reducers(body)

        def end():
            def body():
                @pl.when(diag)
                def _():
                    take(recv1.at[0, pl.ds(0, C - 1)], sbs.at[s])

                @pl.when(jnp.logical_not(diag))
                def _():
                    take(recv1.at[0], sbs.at[s])
            reducers(body)
        ends.append(end)

    def times_rows(name, s, emit):
        slot = ready(name)
        left = stacked(jnp.concatenate([gat[s, q] for q in range(nred)], axis=1))

        def step(j, _):
            t = far_first(j)
            high, low = split_rows(wbuf[slot, pl.ds(pl.multiple_of(t * CH, CH), CH), :])
            dims = (((1,), (1,)), ((), ()))
            both = lax.dot_general(left, high, dims, preferred_element_type=jnp.float32)
            both += lax.dot_general(left, low, dims, preferred_element_type=jnp.float32)
            n = both.shape[0] // 2
            emit(t, both[:n] + both[n:])
            return 0

        lax.fori_loop(0, NT, step, 0)
        used(name)

    def times_cols(name, s, arriving=False):
        slot = ready(name)
        n = rowb.shape[2]

        def step(j, total):
            t = far_first(NT - 1 - j)
            if arriving:
                take(rowb.at[s, t], sbr.at[s, t])
            left = stacked(rowb[s, t])
            high, low = split_rows(wbuf[slot, pl.ds(pl.multiple_of(t * CH, CH), CH), :])
            total += jnp.dot(left, high, preferred_element_type=jnp.float32)
            return total + jnp.dot(left, low, preferred_element_type=jnp.float32)

        total = lax.fori_loop(0, NT, step, jnp.zeros((2 * n, W), jnp.float32))
        used(name)
        return total[:n] + total[n:]

    @pl.when(diag)
    def _():
        for q in range(nred):
            gat[0, q] = rhs_ref[0, :, pl.ds(pl.multiple_of(part * W + q * CH, CH), CH)]
        for d in range(1, R):
            remote(gat.at[0], gat.at[0], s2s.at[0], s2r.at[0], lax.rem(r + d, R), c).start()

    def end_first():
        @pl.when(diag)
        def _():
            take(xr.at[pl.ds(0, R - 1)], s2s.at[0])
    ends.append(end_first)
    own = c == r * ratio
    for k in range(1, count):
        for t in range(NT):
            pend[k, t] = jnp.where(own, rhs_ref[k, :, t * CH:(t + 1) * CH], 0.0)

    @pl.when(jnp.logical_not(diag))
    def _():
        take(gat.at[0], s2r.at[0])

    late = []

    def fill_late():
        if late:
            i, k, s = late.pop(0)

            def emit(t, value, i=i):
                pend[i, t] = pend[i, t] - value
            times_rows(L(i, k), s, emit)

    col_at = 0
    stage = 0
    for k in range(count):
        def emit(t, value, s=stage):
            send1[s, t] = value
            scatter_tile(s, t)
        times_rows(M(k), col_at, emit)
        scatter_rows_ends(stage)
        prefetch(2)
        fill_late()
        entry = stage + 1
        sum_rows(stage, entry)
        stage += 1
        if k == count - 1:
            break
        gather_start(gat.at[entry], s2s.at[entry], s2r.at[entry])
        gather_wait(gat.at[entry], s2r.at[entry])
        late = late + [(i, k, entry) for i in range(k + 2, count)]

        def emit_l(t, value, s=stage, i=k + 1):
            send1[s, t] = pend[i, t] - value
            scatter_tile(s, t)
        times_rows(L(k + 1, k), entry, emit_l)
        scatter_rows_ends(stage)
        prefetch(2)
        late.sort(key=lambda n: n[0])
        fill_late()
        entry = stage + 1
        sum_rows(stage, entry)
        gather_start(gat.at[entry], s2s.at[entry], s2r.at[entry])
        gather_wait(gat.at[entry], s2r.at[entry])
        col_at = entry
        stage += 1

    def pivot(k):
        return piv_ref[k:k + 1, pl.ds(pl.multiple_of(c * W + r * CH, CH), CH)]

    n_cols = 0
    n_rows = 0

    def scale_last():
        wb[count - 1] = gat[2 * count - 1, r] / pivot(count - 1)
    reducers(scale_last)
    spread_rows(0, wb.at[count - 1])
    n_rows = 1
    blate = []

    def fill_blate():
        if blate:
            i, j, s = blate.pop(0)
            total = times_cols(L(i, j), s)
            if i == count - 1:
                bpend[j] = total
            else:
                bpend[j] = bpend[j] + total

    def put_cols(total, s):
        for q in range(nred):
            senda[s, q] = total[:, q * CH:(q + 1) * CH]

    for k in reversed(range(count)):
        prefetch(2)
        fill_blate()
        total = times_cols(M(k), n_rows - 1, True)
        if k == 0:
            for q in range(nred):
                xs[q] = total[:, q * CH:(q + 1) * CH]
            for d in range(1, R):
                remote(xs, xr.at[r], sfs.at[0], sfr.at[0], lax.rem(r + d, R), c).start()
            xr[r] = xs[...]
            break
        put_cols(total, n_cols)
        scatter_cols(n_cols)
        prefetch(2)

        def keep_answer(k=k, s=n_cols):
            xg[k, r] = sum_cols(s)
        reducers(keep_answer)
        n_cols += 1
        spread_rows(n_rows, xg.at[k, r])
        n_rows += 1
        gather_start(xg.at[k], sxs.at[k], sxr.at[k])
        fill_blate()
        total = times_cols(L(k, k - 1), n_rows - 1, True)
        if k < count - 1:
            total = bpend[k - 1] + total
        put_cols(total, n_cols)
        scatter_cols(n_cols)
        prefetch(2)

        def scale(k=k, s=n_cols):
            wb[k - 1] = gat[2 * k - 1, r] / pivot(k - 1) - sum_cols(s)
        reducers(scale)
        n_cols += 1
        spread_rows(n_rows, wb.at[k - 1])
        n_rows += 1
        blate = blate + [(k, j, n_rows - 2) for j in reversed(range(k - 1))]
        blate.sort(key=lambda n: -n[1])

    for k in range(1, count):
        gather_wait(xg.at[k], sxr.at[k])
        for q in range(nred):
            out_ref[k, :, q * CH:(q + 1) * CH] = xg[k, q]
    for end in ends:
        end()
    take(xr.at[pl.ds(0, R - 1)], sfr.at[0])
    summed = jnp.sum(xr[...], axis=0)
    for q in range(nred):
        out_ref[0, :, q * CH:(q + 1) * CH] = summed[q]
    take(xr.at[pl.ds(0, R - 1)], sfs.at[0])
    assert position[0] == len(uses)


def local(R, C, rhs, off_blocks, inverse_blocks, pivots):
    count, rows_tile, W = inverse_blocks.shape
    n = rhs.shape[1]
    nred = max(1, min(R, W // 128))
    CH = W // nred
    NT = rows_tile // CH
    f32 = jnp.float32
    blocks = count + off_blocks.shape[0]
    slots = min(blocks, (56 << 20) // (rows_tile * W * 4))
    dma = pltpu.SemaphoreType.DMA
    vmem = pl.BlockSpec(memory_space=pltpu.VMEM)
    hbm = pl.BlockSpec(memory_space=pl.ANY)
    return pl.pallas_call(
        functools.partial(kernel, R, C),
        out_shape=jax.ShapeDtypeStruct((count, n, W), f32),
        in_specs=[vmem, vmem, hbm, hbm],
        out_specs=vmem,
        scratch_shapes=[
            pltpu.VMEM((slots, rows_tile, W), f32),
            pltpu.VMEM((count, NT, n, CH), f32),
            pltpu.VMEM((count, n, W), f32),
            pltpu.VMEM((count, n, CH), f32),
            pltpu.VMEM((2 * count - 1, NT, n, CH), f32),
            pltpu.VMEM((2 * count - 1, C, n, CH), f32),
            pltpu.VMEM((2 * count, nred, n, CH), f32),
            pltpu.VMEM((2 * count - 2, nred, n, CH), f32),
            pltpu.VMEM((2 * count - 2, R, n, CH), f32),
            pltpu.VMEM((2 * count - 1, NT, n, CH), f32),
            pltpu.VMEM((count, nred, n, CH), f32),
            pltpu.VMEM((nred, n, CH), f32),
            pltpu.VMEM((R, nred, n, CH), f32),
            dma((2 * blocks,)),
            dma((2 * count - 1,)), dma((2 * count - 1,)),
            dma((2 * count,)), dma((2 * count,)),
            dma((2 * count - 2,)), dma((2 * count - 2,)),
            dma((2 * count - 1,)), dma((2 * count - 1, NT)),
            dma((count,)), dma((count,)),
            dma((1,)), dma((1,)),
        ],
        compiler_params=pltpu.CompilerParams(
            collective_id=0, has_side_effects=True, vmem_limit_bytes=67043328),
    )(rhs, pivots, off_blocks, inverse_blocks)


def solution(mesh):
    return jax.shard_map(
        functools.partial(local, mesh.shape["row"], mesh.shape["col"]),
        mesh=mesh,
        in_specs=(P(None, None, "row"), P(None, "row", "col"), P(None, "row", "col"), P()),
        out_specs=P(None, None, "col"),
        check_vma=False,
    )
```

```python
import functools

import jax
import jax.numpy as jnp
from jax import lax
from jax.experimental import pallas as pl
from jax.experimental.pallas import tpu as pltpu
from jax.sharding import PartitionSpec as P

MESH = pl.DeviceIdType.MESH


def block_slot(target, source, count):
    return source * count - source * (source + 1) // 2 + (target - source - 1)


def split_rows(value):
    high = value.astype(jnp.bfloat16)
    low = (value - high.astype(jnp.float32)).astype(jnp.bfloat16)
    return high, low


def stacked(value):
    high = value.astype(jnp.bfloat16).astype(jnp.float32)
    return jnp.concatenate([high, value - high], axis=0).astype(jnp.bfloat16)


def kernel(R, C, rhs_ref, piv_ref, off_ref, inv_ref, out_ref,
           wbuf, pend, bpend, wb, send1, recv1, gat, senda, recva, rowb, xg, xs, xr,
           load_sem, s1s, s1r, s2s, s2r, sas, sar, sbs, sbr, sxs, sxr, sfs, sfr):
    count = inv_ref.shape[0]
    W = inv_ref.shape[2]
    ratio = C // R
    nred, CH = gat.shape[1], gat.shape[3]
    NT = ratio * nred
    GROUP = 2 if NT % 2 == 0 else 1
    r = lax.axis_index("row")
    c = lax.axis_index("col")
    home = c // ratio
    part = c % ratio
    diag = r == home

    def source(name):
        kind, i, k = name
        if kind == "m":
            return inv_ref.at[k]
        return off_ref.at[block_slot(i, k, count)]

    where = {}
    load_id = [0]
    waiting = {}

    def load(name, slot):
        copy = pltpu.make_async_copy(source(name), wbuf.at[slot], load_sem.at[load_id[0]])
        load_id[0] += 1
        copy.start()
        for old in [n for n, s in where.items() if s == slot]:
            del where[old]
        where[name] = slot
        waiting[name] = copy

    def ready(name):
        if name in waiting:
            waiting.pop(name).wait()
        return where[name]

    M = lambda k: ("m", k, k)
    L = lambda i, k: ("l", i, k)
    slots = wbuf.shape[0]

    uses = []
    late = []
    for k in range(count):
        uses.append(M(k))
        if late:
            uses.append(late.pop(0))
        if k + 1 < count:
            uses.append(L(k + 1, k))
        late = late + [L(i, k) for i in range(k + 2, count)]
        late.sort(key=lambda n: n[1])
        if late:
            uses.append(late.pop(0))
    blate = []
    for k in reversed(range(count)):
        uses.append(M(k))
        if blate:
            uses.append(blate.pop(0))
        if k > 0:
            uses.append(L(k, k - 1))
        blate = blate + [L(k, j) for j in reversed(range(k - 1))]
        blate.sort(key=lambda n: -n[2])
        if blate:
            uses.append(blate.pop(0))
    position = [0]

    def prefetch(most):
        now = position[0]
        started = 0
        for at in range(now, len(uses)):
            name = uses[at]
            if name in where:
                continue
            free = [s for s in range(slots) if s not in where.values()]
            if free:
                slot = free[0]
            else:
                def next_use(n):
                    later = [u for u in range(now, len(uses)) if uses[u] == n]
                    return later[0] if later else len(uses) + 1
                victim = max(where, key=next_use)
                if next_use(victim) <= at or victim in waiting:
                    return
                slot = where[victim]
            load(name, slot)
            started += 1
            if started == most:
                return

    def used(name):
        assert uses[position[0]] == name
        position[0] += 1

    prefetch(1)

    barrier = pltpu.get_barrier_semaphore()

    def greet(row, col):
        @pl.when(jnp.logical_not(jnp.logical_and(row == r, col == c)))
        def _():
            pl.semaphore_signal(barrier, inc=1, device_id=(row, col), device_id_type=MESH)

    for h in range(ratio):
        for q in range(R):
            greet(jnp.int32(q), r * ratio + h)
    for cc in range(C):
        greet(home, jnp.int32(cc))
    for d in range(1, R):
        pl.semaphore_signal(barrier, inc=1, device_id=(lax.rem(r + d, R), c), device_id_type=MESH)
    pl.semaphore_wait(barrier, ratio * R + C + R - 1 - 2 * diag.astype(jnp.int32))

    def remote(src, dst, ssem, rsem, row, col):
        return pltpu.make_async_remote_copy(
            src_ref=src, dst_ref=dst, send_sem=ssem, recv_sem=rsem,
            device_id=(row, col), device_id_type=MESH)

    def take(ref, sem):
        pltpu.make_async_copy(ref, ref, sem).wait()

    def reducers(body):
        if nred == R:
            body()
        else:
            pl.when(r < nred)(body)

    ends = []

    def send_or_keep(src, dst, ssem, rsem, row, col):
        same = jnp.logical_and(row == r, col == c)

        @pl.when(same)
        def _():
            pltpu.make_async_copy(src, dst, rsem).start()

        @pl.when(jnp.logical_not(same))
        def _():
            remote(src, dst, ssem, rsem, row, col).start()

    def far_first(j):
        at = lax.rem(j, nred)
        q = at
        if nred % 2 == 0:
            chip = lax.rem(r // 2 + 1 + at // 2, nred // 2)
            q = chip * 2 + lax.rem(r + 1 + at, 2)
        return lax.rem(part + 1 + j // nred, ratio) * nred + q

    def scatter_tile(s, t):
        send_or_keep(send1.at[s, t], recv1.at[s, c], s1s.at[s], s1r.at[s],
                     lax.rem(t, nred), r * ratio + t // nred)

    def scatter_rows_ends(s):
        def end():
            kept = jnp.logical_and(diag, r < nred)

            @pl.when(kept)
            def _():
                take(send1.at[s, pl.ds(0, NT - 1)], s1s.at[s])

            @pl.when(jnp.logical_not(kept))
            def _():
                take(send1.at[s], s1s.at[s])
        ends.append(end)

    def sum_rows(s, entry):
        def body():
            take(recv1.at[s], s1r.at[s])
            gat[entry, r] = jnp.sum(recv1[s], axis=0)
        reducers(body)

    def gather_start(buf, ssem, rsem):
        def body():
            for d in range(1, R):
                remote(buf.at[r], buf.at[r], ssem, rsem, lax.rem(r + d, R), c).start()
        reducers(body)

        def end():
            def body():
                for_all = recva.at[0, pl.ds(0, R - 1)]
                take(for_all, ssem)
            reducers(body)
        ends.append(end)

    def gather_wait(buf, rsem):
        if nred == R:
            take(buf.at[pl.ds(0, nred - 1)], rsem)
        else:
            @pl.when(r < nred)
            def _():
                take(buf.at[pl.ds(0, nred - 1)], rsem)

            @pl.when(r >= nred)
            def _():
                take(buf, rsem)

    def scatter_cols(s):
        for d in range(1, R):
            q = lax.rem(r + d, R)

            def body(q=q):
                remote(senda.at[s, q], recva.at[s, r], sas.at[s], sar.at[s], q, c).start()
            if nred == R:
                body()
            else:
                pl.when(q < nred)(body)

        def keep():
            recva[s, r] = senda[s, r]
        reducers(keep)

        def end():
            gather_wait(senda.at[s], sas.at[s])
        ends.append(end)

    def sum_cols(s):
        take(recva.at[s, pl.ds(0, R - 1)], sar.at[s])
        return jnp.sum(recva[s], axis=0)

    def spread_rows(s, src):
        def body():
            slot = part * nred + r
            upper = c // (C // 2)
            for j in range(C):
                cc = upper * j + (1 - upper) * (C - 1 - j)
                send_or_keep(src, rowb.at[s, slot], sbs.at[s], sbr.at[s, slot], home, cc)
        reducers(body)

        def end():
            def body():
                @pl.when(diag)
                def _():
                    take(recv1.at[0, pl.ds(0, C - 1)], sbs.at[s])

                @pl.when(jnp.logical_not(diag))
                def _():
                    take(recv1.at[0], sbs.at[s])
            reducers(body)
        ends.append(end)

    def times_rows(name, s, emit):
        slot = ready(name)
        left = stacked(jnp.concatenate([gat[s, q] for q in range(nred)], axis=1))

        def step(i, _):
            tiles = [far_first(i * GROUP + g) for g in range(GROUP)]
            values = []
            for t in tiles:
                high, low = split_rows(wbuf[slot, pl.ds(pl.multiple_of(t * CH, CH), CH), :])
                dims = (((1,), (1,)), ((), ()))
                both = lax.dot_general(left, high, dims, preferred_element_type=jnp.float32)
                both += lax.dot_general(left, low, dims, preferred_element_type=jnp.float32)
                n = both.shape[0] // 2
                values.append(both[:n] + both[n:])
            for t, value in zip(tiles, values):
                emit(t, value)
            return 0

        lax.fori_loop(0, NT // GROUP, step, 0)
        used(name)

    def times_cols(name, s, arriving=False):
        slot = ready(name)
        n = rowb.shape[2]

        def step(i, total):
            tiles = [far_first(NT - 1 - (i * GROUP + g)) for g in range(GROUP)]
            if arriving:
                for t in tiles:
                    take(rowb.at[s, t], sbr.at[s, t])
            for t in tiles:
                left = stacked(rowb[s, t])
                high, low = split_rows(wbuf[slot, pl.ds(pl.multiple_of(t * CH, CH), CH), :])
                total += jnp.dot(left, high, preferred_element_type=jnp.float32)
                total += jnp.dot(left, low, preferred_element_type=jnp.float32)
            return total

        total = lax.fori_loop(0, NT // GROUP, step, jnp.zeros((2 * n, W), jnp.float32))
        used(name)
        return total[:n] + total[n:]

    @pl.when(diag)
    def _():
        for q in range(nred):
            gat[0, q] = rhs_ref[0, :, pl.ds(pl.multiple_of(part * W + q * CH, CH), CH)]
        for d in range(1, R):
            remote(gat.at[0], gat.at[0], s2s.at[0], s2r.at[0], lax.rem(r + d, R), c).start()

    def end_first():
        @pl.when(diag)
        def _():
            take(xr.at[pl.ds(0, R - 1)], s2s.at[0])
    ends.append(end_first)
    own = c == r * ratio
    for k in range(1, count):
        for t in range(NT):
            pend[k, t] = jnp.where(own, rhs_ref[k, :, t * CH:(t + 1) * CH], 0.0)

    prefetch(2)

    @pl.when(jnp.logical_not(diag))
    def _():
        take(gat.at[0], s2r.at[0])

    late = []

    def fill_late():
        if late:
            i, k, s = late.pop(0)

            def emit(t, value, i=i):
                pend[i, t] = pend[i, t] - value
            times_rows(L(i, k), s, emit)

    col_at = 0
    stage = 0
    for k in range(count):
        def emit(t, value, s=stage):
            send1[s, t] = value
            scatter_tile(s, t)
        times_rows(M(k), col_at, emit)
        scatter_rows_ends(stage)
        prefetch(2)
        fill_late()
        entry = stage + 1
        sum_rows(stage, entry)
        stage += 1
        if k == count - 1:
            break
        gather_start(gat.at[entry], s2s.at[entry], s2r.at[entry])
        gather_wait(gat.at[entry], s2r.at[entry])
        late = late + [(i, k, entry) for i in range(k + 2, count)]

        def emit_l(t, value, s=stage, i=k + 1):
            send1[s, t] = pend[i, t] - value
            scatter_tile(s, t)
        times_rows(L(k + 1, k), entry, emit_l)
        scatter_rows_ends(stage)
        prefetch(2)
        late.sort(key=lambda n: n[0])
        fill_late()
        entry = stage + 1
        sum_rows(stage, entry)
        gather_start(gat.at[entry], s2s.at[entry], s2r.at[entry])
        gather_wait(gat.at[entry], s2r.at[entry])
        col_at = entry
        stage += 1

    def pivot(k):
        return piv_ref[k:k + 1, pl.ds(pl.multiple_of(c * W + r * CH, CH), CH)]

    n_cols = 0
    n_rows = 0

    def scale_last():
        wb[count - 1] = gat[2 * count - 1, r] / pivot(count - 1)
    reducers(scale_last)
    spread_rows(0, wb.at[count - 1])
    n_rows = 1
    blate = []

    def fill_blate():
        if blate:
            i, j, s = blate.pop(0)
            total = times_cols(L(i, j), s)
            if i == count - 1:
                bpend[j] = total
            else:
                bpend[j] = bpend[j] + total

    def put_cols(total, s):
        for q in range(nred):
            senda[s, q] = total[:, q * CH:(q + 1) * CH]

    for k in reversed(range(count)):
        prefetch(2)
        fill_blate()
        total = times_cols(M(k), n_rows - 1, True)
        if k == 0:
            for q in range(nred):
                xs[q] = total[:, q * CH:(q + 1) * CH]
            for d in range(1, R):
                remote(xs, xr.at[r], sfs.at[0], sfr.at[0], lax.rem(r + d, R), c).start()
            xr[r] = xs[...]
            break
        put_cols(total, n_cols)
        scatter_cols(n_cols)
        prefetch(2)

        def keep_answer(k=k, s=n_cols):
            xg[k, r] = sum_cols(s)
        reducers(keep_answer)
        n_cols += 1
        spread_rows(n_rows, xg.at[k, r])
        n_rows += 1
        gather_start(xg.at[k], sxs.at[k], sxr.at[k])
        fill_blate()
        total = times_cols(L(k, k - 1), n_rows - 1, True)
        if k < count - 1:
            total = bpend[k - 1] + total
        put_cols(total, n_cols)
        scatter_cols(n_cols)
        prefetch(2)

        def scale(k=k, s=n_cols):
            wb[k - 1] = gat[2 * k - 1, r] / pivot(k - 1) - sum_cols(s)
        reducers(scale)
        n_cols += 1
        spread_rows(n_rows, wb.at[k - 1])
        n_rows += 1
        blate = blate + [(k, j, n_rows - 2) for j in reversed(range(k - 1))]
        blate.sort(key=lambda n: -n[1])

    for k in range(1, count):
        gather_wait(xg.at[k], sxr.at[k])
        for q in range(nred):
            out_ref[k, :, q * CH:(q + 1) * CH] = xg[k, q]
    for end in ends:
        end()
    take(xr.at[pl.ds(0, R - 1)], sfr.at[0])
    summed = jnp.sum(xr[...], axis=0)
    for q in range(nred):
        out_ref[0, :, q * CH:(q + 1) * CH] = summed[q]
    take(xr.at[pl.ds(0, R - 1)], sfs.at[0])
    assert position[0] == len(uses)


def local(R, C, rhs, off_blocks, inverse_blocks, pivots):
    count, rows_tile, W = inverse_blocks.shape
    n = rhs.shape[1]
    nred = max(1, min(R, W // 128))
    CH = W // nred
    NT = rows_tile // CH
    f32 = jnp.float32
    blocks = count + off_blocks.shape[0]
    slots = min(blocks, (56 << 20) // (rows_tile * W * 4))
    dma = pltpu.SemaphoreType.DMA
    vmem = pl.BlockSpec(memory_space=pltpu.VMEM)
    hbm = pl.BlockSpec(memory_space=pl.ANY)
    return pl.pallas_call(
        functools.partial(kernel, R, C),
        out_shape=jax.ShapeDtypeStruct((count, n, W), f32),
        in_specs=[vmem, vmem, hbm, hbm],
        out_specs=vmem,
        scratch_shapes=[
            pltpu.VMEM((slots, rows_tile, W), f32),
            pltpu.VMEM((count, NT, n, CH), f32),
            pltpu.VMEM((count, n, W), f32),
            pltpu.VMEM((count, n, CH), f32),
            pltpu.VMEM((2 * count - 1, NT, n, CH), f32),
            pltpu.VMEM((2 * count - 1, C, n, CH), f32),
            pltpu.VMEM((2 * count, nred, n, CH), f32),
            pltpu.VMEM((2 * count - 2, nred, n, CH), f32),
            pltpu.VMEM((2 * count - 2, R, n, CH), f32),
            pltpu.VMEM((2 * count - 1, NT, n, CH), f32),
            pltpu.VMEM((count, nred, n, CH), f32),
            pltpu.VMEM((nred, n, CH), f32),
            pltpu.VMEM((R, nred, n, CH), f32),
            dma((2 * blocks,)),
            dma((2 * count - 1,)), dma((2 * count - 1,)),
            dma((2 * count,)), dma((2 * count,)),
            dma((2 * count - 2,)), dma((2 * count - 2,)),
            dma((2 * count - 1,)), dma((2 * count - 1, NT)),
            dma((count,)), dma((count,)),
            dma((1,)), dma((1,)),
        ],
        compiler_params=pltpu.CompilerParams(
            collective_id=0, has_side_effects=True, vmem_limit_bytes=67043328),
    )(rhs, pivots, off_blocks, inverse_blocks)


def solution(mesh):
    return jax.shard_map(
        functools.partial(local, mesh.shape["row"], mesh.shape["col"]),
        mesh=mesh,
        in_specs=(P(None, None, "row"), P(None, "row", "col"), P(None, "row", "col"), P()),
        out_specs=P(None, None, "col"),
        check_vma=False,
    )
```

```python
import functools

import jax
import jax.numpy as jnp
from jax import lax
from jax.experimental import pallas as pl
from jax.experimental.pallas import tpu as pltpu
from jax.sharding import PartitionSpec as P

MESH = pl.DeviceIdType.MESH


def block_slot(target, source, count):
    return source * count - source * (source + 1) // 2 + (target - source - 1)


def split_rows(value):
    high = value.astype(jnp.bfloat16)
    low = (value - high.astype(jnp.float32)).astype(jnp.bfloat16)
    return high, low


def stacked(value):
    high = value.astype(jnp.bfloat16).astype(jnp.float32)
    return jnp.concatenate([high, value - high], axis=0).astype(jnp.bfloat16)


def kernel(R, C, rhs_ref, piv_ref, off_ref, inv_ref, out_ref,
           wbuf, partial, pend, bpend, wb, send1, recv1, gat, senda, recva, rowb, xg, xs, xr,
           load_sem, s1s, s1r, s2s, s2r, sas, sar, sbs, sbr, sxs, sxr, sfs, sfr):
    count = inv_ref.shape[0]
    W = inv_ref.shape[2]
    ratio = C // R
    nred, CH = gat.shape[1], gat.shape[3]
    NT = ratio * nred
    GROUP = 2 if NT % 2 == 0 else 1
    r = lax.axis_index("row")
    c = lax.axis_index("col")
    home = c // ratio
    part = c % ratio
    diag = r == home

    def source(name):
        kind, i, k = name
        if kind == "m":
            return inv_ref.at[k]
        return off_ref.at[block_slot(i, k, count)]

    where = {}
    load_id = [0]
    waiting = {}

    def load(name, slot):
        copy = pltpu.make_async_copy(source(name), wbuf.at[slot], load_sem.at[load_id[0]])
        load_id[0] += 1
        copy.start()
        for old in [n for n, s in where.items() if s == slot]:
            del where[old]
        where[name] = slot
        waiting[name] = copy

    def ready(name):
        if name in waiting:
            waiting.pop(name).wait()
        return where[name]

    M = lambda k: ("m", k, k)
    L = lambda i, k: ("l", i, k)
    slots = wbuf.shape[0]

    uses = []
    late = []
    for k in range(count):
        uses.append(M(k))
        if late:
            uses.append(late.pop(0))
        if k + 1 < count:
            uses.append(L(k + 1, k))
        late = late + [L(i, k) for i in range(k + 2, count)]
        late.sort(key=lambda n: n[1])
        if late:
            uses.append(late.pop(0))
    blate = []
    for k in reversed(range(count)):
        uses.append(M(k))
        if blate:
            uses.append(blate.pop(0))
        if k > 0:
            uses.append(L(k, k - 1))
        blate = blate + [L(k, j) for j in reversed(range(k - 1))]
        blate.sort(key=lambda n: -n[2])
        if blate:
            uses.append(blate.pop(0))
    position = [0]

    def prefetch(most):
        now = position[0]
        started = 0
        for at in range(now, len(uses)):
            name = uses[at]
            if name in where:
                continue
            free = [s for s in range(slots) if s not in where.values()]
            if free:
                slot = free[0]
            else:
                def next_use(n):
                    later = [u for u in range(now, len(uses)) if uses[u] == n]
                    return later[0] if later else len(uses) + 1
                victim = max(where, key=next_use)
                if next_use(victim) <= at or victim in waiting:
                    return
                slot = where[victim]
            load(name, slot)
            started += 1
            if started == most:
                return

    def used(name):
        assert uses[position[0]] == name
        position[0] += 1

    prefetch(1)

    barrier = pltpu.get_barrier_semaphore()

    def greet(row, col):
        @pl.when(jnp.logical_not(jnp.logical_and(row == r, col == c)))
        def _():
            pl.semaphore_signal(barrier, inc=1, device_id=(row, col), device_id_type=MESH)

    for h in range(ratio):
        for q in range(R):
            greet(jnp.int32(q), r * ratio + h)
    for cc in range(C):
        greet(home, jnp.int32(cc))
    for d in range(1, R):
        pl.semaphore_signal(barrier, inc=1, device_id=(lax.rem(r + d, R), c), device_id_type=MESH)
    pl.semaphore_wait(barrier, ratio * R + C + R - 1 - 2 * diag.astype(jnp.int32))

    def remote(src, dst, ssem, rsem, row, col):
        return pltpu.make_async_remote_copy(
            src_ref=src, dst_ref=dst, send_sem=ssem, recv_sem=rsem,
            device_id=(row, col), device_id_type=MESH)

    def take(ref, sem):
        pltpu.make_async_copy(ref, ref, sem).wait()

    def reducers(body):
        if nred == R:
            body()
        else:
            pl.when(r < nred)(body)

    ends = []

    def send_or_keep(src, dst, ssem, rsem, row, col):
        same = jnp.logical_and(row == r, col == c)

        @pl.when(same)
        def _():
            pltpu.make_async_copy(src, dst, rsem).start()

        @pl.when(jnp.logical_not(same))
        def _():
            remote(src, dst, ssem, rsem, row, col).start()

    def far_first(j):
        at = lax.rem(j, nred)
        q = at
        if nred % 2 == 0:
            chip = lax.rem(r // 2 + 1 + at // 2, nred // 2)
            q = chip * 2 + lax.rem(r + 1 + at, 2)
        return lax.rem(part + 1 + j // nred, ratio) * nred + q

    def scatter_tile(s, t):
        send_or_keep(send1.at[s, t], recv1.at[s, c], s1s.at[s], s1r.at[s],
                     lax.rem(t, nred), r * ratio + t // nred)

    def scatter_rows_ends(s):
        def end():
            kept = jnp.logical_and(diag, r < nred)

            @pl.when(kept)
            def _():
                take(send1.at[s, pl.ds(0, NT - 1)], s1s.at[s])

            @pl.when(jnp.logical_not(kept))
            def _():
                take(send1.at[s], s1s.at[s])
        ends.append(end)

    def sum_rows(s, entry):
        def body():
            take(recv1.at[s], s1r.at[s])
            gat[entry, r] = jnp.sum(recv1[s], axis=0)
        reducers(body)

    def gather_start(buf, ssem, rsem):
        def body():
            for d in range(1, R):
                remote(buf.at[r], buf.at[r], ssem, rsem, lax.rem(r + d, R), c).start()
        reducers(body)

        def end():
            def body():
                for_all = recva.at[0, pl.ds(0, R - 1)]
                take(for_all, ssem)
            reducers(body)
        ends.append(end)

    def gather_wait(buf, rsem):
        if nred == R:
            take(buf.at[pl.ds(0, nred - 1)], rsem)
        else:
            @pl.when(r < nred)
            def _():
                take(buf.at[pl.ds(0, nred - 1)], rsem)

            @pl.when(r >= nred)
            def _():
                take(buf, rsem)

    def scatter_cols(s):
        for d in range(1, R):
            q = lax.rem(r + d, R)

            def body(q=q):
                remote(senda.at[s, q], recva.at[s, r], sas.at[s], sar.at[s], q, c).start()
            if nred == R:
                body()
            else:
                pl.when(q < nred)(body)

        def keep():
            recva[s, r] = senda[s, r]
        reducers(keep)

        def end():
            gather_wait(senda.at[s], sas.at[s])
        ends.append(end)

    def sum_cols(s):
        take(recva.at[s, pl.ds(0, R - 1)], sar.at[s])
        return jnp.sum(recva[s], axis=0)

    def spread_rows(s, src):
        def body():
            slot = part * nred + r
            upper = c // (C // 2)
            for j in range(C):
                cc = upper * j + (1 - upper) * (C - 1 - j)
                send_or_keep(src, rowb.at[s, slot], sbs.at[s], sbr.at[s, slot], home, cc)
        reducers(body)

        def end():
            def body():
                @pl.when(diag)
                def _():
                    take(recv1.at[0, pl.ds(0, C - 1)], sbs.at[s])

                @pl.when(jnp.logical_not(diag))
                def _():
                    take(recv1.at[0], sbs.at[s])
            reducers(body)
        ends.append(end)

    def times_rows(name, s, emit):
        slot = ready(name)
        left = stacked(jnp.concatenate([gat[s, q] for q in range(nred)], axis=1))

        def step(i, _):
            tiles = [far_first(i * GROUP + g) for g in range(GROUP)]
            values = []
            for t in tiles:
                high, low = split_rows(wbuf[slot, pl.ds(pl.multiple_of(t * CH, CH), CH), :])
                dims = (((1,), (1,)), ((), ()))
                both = lax.dot_general(left, high, dims, preferred_element_type=jnp.float32)
                both += lax.dot_general(left, low, dims, preferred_element_type=jnp.float32)
                n = both.shape[0] // 2
                values.append(both[:n] + both[n:])
            for t, value in zip(tiles, values):
                emit(t, value)
            return 0

        lax.fori_loop(0, NT // GROUP, step, 0)
        used(name)

    def times_rows_arriving(name, s, emit):
        if nred != R or R % 2 or R < 4:
            for q in range(nred):
                @pl.when(r != q)
                def _(q=q):
                    take(gat.at[s, q], s2r.at[s, q])
            times_rows(name, s, emit)
            return
        slot = ready(name)
        n = gat.shape[2]
        dims = (((1,), (1,)), ((), ()))
        mate = r + 1 - 2 * lax.rem(r, 2)
        passes = [(r, 1), (mate, 1)]
        for d in range(1, R // 2):
            passes.append((lax.rem(r // 2 + d, R // 2) * 2, 2))
        for at, (first, wide) in enumerate(passes):
            if at > 0:
                for w in range(wide):
                    take(gat.at[s, first + w], s2r.at[s, first + w])
            left = stacked(jnp.concatenate([gat[s, first + w] for w in range(wide)], axis=1))
            lanes = pl.ds(pl.multiple_of(first * CH, CH), wide * CH)
            last = at == len(passes) - 1
            group = GROUP if last or NT % 4 else 4

            def step(i, _, at=at, left=left, lanes=lanes, last=last, group=group):
                tiles = [far_first(i * group + g) for g in range(group)]
                values = []
                for t in tiles:
                    rows = pl.ds(pl.multiple_of(t * CH, CH), CH)
                    high, low = split_rows(wbuf[slot, rows, lanes])
                    both = lax.dot_general(left, high, dims, preferred_element_type=jnp.float32)
                    both += lax.dot_general(left, low, dims, preferred_element_type=jnp.float32)
                    value = both[:n] + both[n:]
                    values.append(value if at == 0 else partial[t] + value)
                for t, value in zip(tiles, values):
                    if last:
                        emit(t, value)
                    else:
                        partial[t] = value
                return 0

            lax.fori_loop(0, NT // group, step, 0)
        used(name)

    def times_cols(name, s, arriving=False):
        slot = ready(name)
        n = rowb.shape[2]

        def step(i, total):
            tiles = [far_first(NT - 1 - (i * GROUP + g)) for g in range(GROUP)]
            if arriving:
                for t in tiles:
                    take(rowb.at[s, t], sbr.at[s, t])
            for t in tiles:
                left = stacked(rowb[s, t])
                high, low = split_rows(wbuf[slot, pl.ds(pl.multiple_of(t * CH, CH), CH), :])
                total += jnp.dot(left, high, preferred_element_type=jnp.float32)
                total += jnp.dot(left, low, preferred_element_type=jnp.float32)
            return total

        total = lax.fori_loop(0, NT // GROUP, step, jnp.zeros((2 * n, W), jnp.float32))
        used(name)
        return total[:n] + total[n:]

    @pl.when(diag)
    def _():
        for q in range(nred):
            gat[0, q] = rhs_ref[0, :, pl.ds(pl.multiple_of(part * W + q * CH, CH), CH)]
        for d in range(1, R):
            remote(gat.at[0], gat.at[0], s2s.at[0], s2r.at[0, 0], lax.rem(r + d, R), c).start()

    def end_first():
        @pl.when(diag)
        def _():
            take(xr.at[pl.ds(0, R - 1)], s2s.at[0])
    ends.append(end_first)
    own = c == r * ratio
    for k in range(1, count):
        for t in range(NT):
            pend[k, t] = jnp.where(own, rhs_ref[k, :, t * CH:(t + 1) * CH], 0.0)

    prefetch(2)

    @pl.when(jnp.logical_not(diag))
    def _():
        take(gat.at[0], s2r.at[0, 0])

    late = []

    def fill_late():
        if late:
            i, k, s = late.pop(0)

            def emit(t, value, i=i):
                pend[i, t] = pend[i, t] - value
            times_rows(L(i, k), s, emit)

    col_at = 0
    stage = 0
    for k in range(count):
        def emit(t, value, s=stage):
            send1[s, t] = value
            scatter_tile(s, t)
        (times_rows if k == 0 else times_rows_arriving)(M(k), col_at, emit)
        scatter_rows_ends(stage)
        prefetch(2)
        fill_late()
        entry = stage + 1
        sum_rows(stage, entry)
        stage += 1
        if k == count - 1:
            break
        gather_start(gat.at[entry], s2s.at[entry], s2r.at[entry, r])
        late = late + [(i, k, entry) for i in range(k + 2, count)]

        def emit_l(t, value, s=stage, i=k + 1):
            send1[s, t] = pend[i, t] - value
            scatter_tile(s, t)
        times_rows_arriving(L(k + 1, k), entry, emit_l)
        scatter_rows_ends(stage)
        prefetch(2)
        late.sort(key=lambda n: n[0])
        fill_late()
        entry = stage + 1
        sum_rows(stage, entry)
        gather_start(gat.at[entry], s2s.at[entry], s2r.at[entry, r])
        col_at = entry
        stage += 1

    def pivot(k):
        return piv_ref[k:k + 1, pl.ds(pl.multiple_of(c * W + r * CH, CH), CH)]

    n_cols = 0
    n_rows = 0

    def scale_last():
        wb[count - 1] = gat[2 * count - 1, r] / pivot(count - 1)
    reducers(scale_last)
    spread_rows(0, wb.at[count - 1])
    n_rows = 1
    blate = []

    def fill_blate():
        if blate:
            i, j, s = blate.pop(0)
            total = times_cols(L(i, j), s)
            if i == count - 1:
                bpend[j] = total
            else:
                bpend[j] = bpend[j] + total

    def put_cols(total, s):
        for q in range(nred):
            senda[s, q] = total[:, q * CH:(q + 1) * CH]

    for k in reversed(range(count)):
        prefetch(2)
        fill_blate()
        total = times_cols(M(k), n_rows - 1, True)
        if k == 0:
            for q in range(nred):
                xs[q] = total[:, q * CH:(q + 1) * CH]
            for d in range(1, R):
                remote(xs, xr.at[r], sfs.at[0], sfr.at[0], lax.rem(r + d, R), c).start()
            xr[r] = xs[...]
            break
        put_cols(total, n_cols)
        scatter_cols(n_cols)
        prefetch(2)

        def keep_answer(k=k, s=n_cols):
            xg[k, r] = sum_cols(s)
        reducers(keep_answer)
        n_cols += 1
        spread_rows(n_rows, xg.at[k, r])
        n_rows += 1
        gather_start(xg.at[k], sxs.at[k], sxr.at[k])
        fill_blate()
        total = times_cols(L(k, k - 1), n_rows - 1, True)
        if k < count - 1:
            total = bpend[k - 1] + total
        put_cols(total, n_cols)
        scatter_cols(n_cols)
        prefetch(2)

        def scale(k=k, s=n_cols):
            wb[k - 1] = gat[2 * k - 1, r] / pivot(k - 1) - sum_cols(s)
        reducers(scale)
        n_cols += 1
        spread_rows(n_rows, wb.at[k - 1])
        n_rows += 1
        blate = blate + [(k, j, n_rows - 2) for j in reversed(range(k - 1))]
        blate.sort(key=lambda n: -n[1])

    for k in range(1, count):
        gather_wait(xg.at[k], sxr.at[k])
        for q in range(nred):
            out_ref[k, :, q * CH:(q + 1) * CH] = xg[k, q]
    for end in ends:
        end()
    take(xr.at[pl.ds(0, R - 1)], sfr.at[0])
    summed = jnp.sum(xr[...], axis=0)
    for q in range(nred):
        out_ref[0, :, q * CH:(q + 1) * CH] = summed[q]
    take(xr.at[pl.ds(0, R - 1)], sfs.at[0])
    assert position[0] == len(uses)


def local(R, C, rhs, off_blocks, inverse_blocks, pivots):
    count, rows_tile, W = inverse_blocks.shape
    n = rhs.shape[1]
    nred = max(1, min(R, W // 128))
    CH = W // nred
    NT = rows_tile // CH
    f32 = jnp.float32
    blocks = count + off_blocks.shape[0]
    slots = min(blocks, (56 << 20) // (rows_tile * W * 4))
    dma = pltpu.SemaphoreType.DMA
    vmem = pl.BlockSpec(memory_space=pltpu.VMEM)
    hbm = pl.BlockSpec(memory_space=pl.ANY)
    return pl.pallas_call(
        functools.partial(kernel, R, C),
        out_shape=jax.ShapeDtypeStruct((count, n, W), f32),
        in_specs=[vmem, vmem, hbm, hbm],
        out_specs=vmem,
        scratch_shapes=[
            pltpu.VMEM((slots, rows_tile, W), f32),
            pltpu.VMEM((NT, n, CH), f32),
            pltpu.VMEM((count, NT, n, CH), f32),
            pltpu.VMEM((count, n, W), f32),
            pltpu.VMEM((count, n, CH), f32),
            pltpu.VMEM((2 * count - 1, NT, n, CH), f32),
            pltpu.VMEM((2 * count - 1, C, n, CH), f32),
            pltpu.VMEM((2 * count, nred, n, CH), f32),
            pltpu.VMEM((2 * count - 2, nred, n, CH), f32),
            pltpu.VMEM((2 * count - 2, R, n, CH), f32),
            pltpu.VMEM((2 * count - 1, NT, n, CH), f32),
            pltpu.VMEM((count, nred, n, CH), f32),
            pltpu.VMEM((nred, n, CH), f32),
            pltpu.VMEM((R, nred, n, CH), f32),
            dma((2 * blocks,)),
            dma((2 * count - 1,)), dma((2 * count - 1,)),
            dma((2 * count,)), dma((2 * count, R)),
            dma((2 * count - 2,)), dma((2 * count - 2,)),
            dma((2 * count - 1,)), dma((2 * count - 1, NT)),
            dma((count,)), dma((count,)),
            dma((1,)), dma((1,)),
        ],
        compiler_params=pltpu.CompilerParams(
            collective_id=0, has_side_effects=True, vmem_limit_bytes=67043328),
    )(rhs, pivots, off_blocks, inverse_blocks)


def solution(mesh):
    return jax.shard_map(
        functools.partial(local, mesh.shape["row"], mesh.shape["col"]),
        mesh=mesh,
        in_specs=(P(None, None, "row"), P(None, "row", "col"), P(None, "row", "col"), P()),
        out_specs=P(None, None, "col"),
        check_vma=False,
    )
```

```python
import functools

import jax
import jax.numpy as jnp
from jax import lax
from jax.experimental import pallas as pl
from jax.experimental.pallas import tpu as pltpu
from jax.sharding import PartitionSpec as P

MESH = pl.DeviceIdType.MESH


def block_slot(target, source, count):
    return source * count - source * (source + 1) // 2 + (target - source - 1)


def split_rows(value):
    high = value.astype(jnp.bfloat16)
    low = (value - high.astype(jnp.float32)).astype(jnp.bfloat16)
    return high, low


def stacked(value):
    high = value.astype(jnp.bfloat16).astype(jnp.float32)
    return jnp.concatenate([high, value - high], axis=0).astype(jnp.bfloat16)


def kernel(R, C, rhs_ref, piv_ref, off_ref, inv_ref, out_ref,
           wbuf, partial, pend, bpend, wb, send1, recv1, gat, senda, recva, rowb, xg, xs, xr,
           load_sem, s1s, s1r, s2s, s2r, sas, sar, sbs, sbr, sxs, sxr, sfs, sfr):
    count = inv_ref.shape[0]
    W = inv_ref.shape[2]
    ratio = C // R
    nred, CH = gat.shape[1], gat.shape[3]
    NT = ratio * nred
    GROUP = 2 if NT % 2 == 0 else 1
    r = lax.axis_index("row")
    c = lax.axis_index("col")
    home = c // ratio
    part = c % ratio
    diag = r == home

    def source(name):
        kind, i, k = name
        if kind == "m":
            return inv_ref.at[k]
        return off_ref.at[block_slot(i, k, count)]

    where = {}
    load_id = [0]
    waiting = {}

    def load(name, slot):
        copy = pltpu.make_async_copy(source(name), wbuf.at[slot], load_sem.at[load_id[0]])
        load_id[0] += 1
        copy.start()
        for old in [n for n, s in where.items() if s == slot]:
            del where[old]
        where[name] = slot
        waiting[name] = copy

    def ready(name):
        if name in waiting:
            waiting.pop(name).wait()
        return where[name]

    M = lambda k: ("m", k, k)
    L = lambda i, k: ("l", i, k)
    slots = wbuf.shape[0]

    uses = []
    late = []
    for k in range(count):
        uses.append(M(k))
        if late:
            uses.append(late.pop(0))
        if k + 1 < count:
            uses.append(L(k + 1, k))
        late = late + [L(i, k) for i in range(k + 2, count)]
        late.sort(key=lambda n: n[1])
        if late:
            uses.append(late.pop(0))
    blate = []
    for k in reversed(range(count)):
        uses.append(M(k))
        if blate:
            uses.append(blate.pop(0))
        if k > 0:
            uses.append(L(k, k - 1))
        blate = blate + [L(k, j) for j in reversed(range(k - 1))]
        blate.sort(key=lambda n: -n[2])
        if blate:
            uses.append(blate.pop(0))
    position = [0]

    def prefetch(most):
        now = position[0]
        started = 0
        for at in range(now, len(uses)):
            name = uses[at]
            if name in where:
                continue
            free = [s for s in range(slots) if s not in where.values()]
            if free:
                slot = free[0]
            else:
                def next_use(n):
                    later = [u for u in range(now, len(uses)) if uses[u] == n]
                    return later[0] if later else len(uses) + 1
                victim = max(where, key=next_use)
                if next_use(victim) <= at or victim in waiting:
                    return
                slot = where[victim]
            load(name, slot)
            started += 1
            if started == most:
                return

    def used(name):
        assert uses[position[0]] == name
        position[0] += 1

    prefetch(1)

    barrier = pltpu.get_barrier_semaphore()

    def greet(row, col):
        @pl.when(jnp.logical_not(jnp.logical_and(row == r, col == c)))
        def _():
            pl.semaphore_signal(barrier, inc=1, device_id=(row, col), device_id_type=MESH)

    for h in range(ratio):
        for q in range(R):
            greet(jnp.int32(q), r * ratio + h)
    for cc in range(C):
        greet(home, jnp.int32(cc))
    for d in range(1, R):
        pl.semaphore_signal(barrier, inc=1, device_id=(lax.rem(r + d, R), c), device_id_type=MESH)
    pl.semaphore_wait(barrier, ratio * R + C + R - 1 - 2 * diag.astype(jnp.int32))

    def remote(src, dst, ssem, rsem, row, col):
        return pltpu.make_async_remote_copy(
            src_ref=src, dst_ref=dst, send_sem=ssem, recv_sem=rsem,
            device_id=(row, col), device_id_type=MESH)

    def take(ref, sem):
        pltpu.make_async_copy(ref, ref, sem).wait()

    def reducers(body):
        if nred == R:
            body()
        else:
            pl.when(r < nred)(body)

    ends = []

    def send_or_keep(src, dst, ssem, rsem, row, col):
        same = jnp.logical_and(row == r, col == c)

        @pl.when(same)
        def _():
            pltpu.make_async_copy(src, dst, rsem).start()

        @pl.when(jnp.logical_not(same))
        def _():
            remote(src, dst, ssem, rsem, row, col).start()

    def far_first(j):
        at = lax.rem(j, nred)
        q = at
        if nred % 2 == 0:
            chip = lax.rem(r // 2 + 1 + at // 2, nred // 2)
            q = chip * 2 + lax.rem(r + 1 + at, 2)
        return lax.rem(part + 1 + j // nred, ratio) * nred + q

    def scatter_tile(s, t):
        send_or_keep(send1.at[s, t], recv1.at[s, c], s1s.at[s], s1r.at[s],
                     lax.rem(t, nred), r * ratio + t // nred)

    def scatter_rows_ends(s):
        def end():
            kept = jnp.logical_and(diag, r < nred)

            @pl.when(kept)
            def _():
                take(send1.at[s, pl.ds(0, NT - 1)], s1s.at[s])

            @pl.when(jnp.logical_not(kept))
            def _():
                take(send1.at[s], s1s.at[s])
        ends.append(end)

    def sum_rows(s, entry):
        def body():
            take(recv1.at[s], s1r.at[s])
            gat[entry, r] = jnp.sum(recv1[s], axis=0)
        reducers(body)

    def gather_start(buf, ssem, rsem):
        def body():
            for d in range(1, R):
                remote(buf.at[r], buf.at[r], ssem, rsem, lax.rem(r + d, R), c).start()
        reducers(body)

        def end():
            def body():
                for_all = recva.at[0, pl.ds(0, R - 1)]
                take(for_all, ssem)
            reducers(body)
        ends.append(end)

    def gather_wait(buf, rsem):
        if nred == R:
            take(buf.at[pl.ds(0, nred - 1)], rsem)
        else:
            @pl.when(r < nred)
            def _():
                take(buf.at[pl.ds(0, nred - 1)], rsem)

            @pl.when(r >= nred)
            def _():
                take(buf, rsem)

    def scatter_cols(s):
        for d in range(1, R):
            q = lax.rem(r + d, R)

            def body(q=q):
                remote(senda.at[s, q], recva.at[s, r], sas.at[s], sar.at[s], q, c).start()
            if nred == R:
                body()
            else:
                pl.when(q < nred)(body)

        def keep():
            recva[s, r] = senda[s, r]
        reducers(keep)

        def end():
            gather_wait(senda.at[s], sas.at[s])
        ends.append(end)

    def sum_cols(s):
        take(recva.at[s, pl.ds(0, R - 1)], sar.at[s])
        return jnp.sum(recva[s], axis=0)

    def spread_rows(s, src):
        def body():
            slot = part * nred + r
            upper = c // (C // 2)
            for j in range(C):
                cc = upper * j + (1 - upper) * (C - 1 - j)
                send_or_keep(src, rowb.at[s, slot], sbs.at[s], sbr.at[s, slot], home, cc)
        reducers(body)

        def end():
            def body():
                @pl.when(diag)
                def _():
                    take(recv1.at[0, pl.ds(0, C - 1)], sbs.at[s])

                @pl.when(jnp.logical_not(diag))
                def _():
                    take(recv1.at[0], sbs.at[s])
            reducers(body)
        ends.append(end)

    def times_rows(name, s, emit):
        slot = ready(name)
        left = stacked(jnp.concatenate([gat[s, q] for q in range(nred)], axis=1))

        def step(i, _):
            tiles = [far_first(i * GROUP + g) for g in range(GROUP)]
            values = []
            for t in tiles:
                high, low = split_rows(wbuf[slot, pl.ds(pl.multiple_of(t * CH, CH), CH), :])
                dims = (((1,), (1,)), ((), ()))
                both = lax.dot_general(left, high, dims, preferred_element_type=jnp.float32)
                both += lax.dot_general(left, low, dims, preferred_element_type=jnp.float32)
                n = both.shape[0] // 2
                values.append(both[:n] + both[n:])
            for t, value in zip(tiles, values):
                emit(t, value)
            return 0

        lax.fori_loop(0, NT // GROUP, step, 0)
        used(name)

    def times_rows_arriving(name, s, emit):
        if nred != R or R % 2 or R < 4:
            for q in range(nred):
                @pl.when(r != q)
                def _(q=q):
                    take(gat.at[s, q], s2r.at[s, q])
            times_rows(name, s, emit)
            return
        slot = ready(name)
        n = gat.shape[2]
        dims = (((1,), (1,)), ((), ()))
        mate = r + 1 - 2 * lax.rem(r, 2)
        passes = [(r, 1), (mate, 1)]
        for d in range(1, R // 2):
            passes.append((lax.rem(r // 2 + d, R // 2) * 2, 2))
        for at, (first, wide) in enumerate(passes):
            if at > 0:
                for w in range(wide):
                    take(gat.at[s, first + w], s2r.at[s, first + w])
            left = stacked(jnp.concatenate([gat[s, first + w] for w in range(wide)], axis=1))
            lanes = pl.ds(pl.multiple_of(first * CH, CH), wide * CH)
            last = at == len(passes) - 1
            group = GROUP if last or NT > 8 else NT

            def step(i, _, at=at, left=left, lanes=lanes, last=last, group=group):
                tiles = [far_first(i * group + g) for g in range(group)]
                values = []
                for t in tiles:
                    rows = pl.ds(pl.multiple_of(t * CH, CH), CH)
                    high, low = split_rows(wbuf[slot, rows, lanes])
                    both = lax.dot_general(left, high, dims, preferred_element_type=jnp.float32)
                    both += lax.dot_general(left, low, dims, preferred_element_type=jnp.float32)
                    value = both[:n] + both[n:]
                    values.append(value if at == 0 else partial[t] + value)
                for t, value in zip(tiles, values):
                    if last:
                        emit(t, value)
                    else:
                        partial[t] = value
                return 0

            lax.fori_loop(0, NT // group, step, 0)
        used(name)

    def times_cols(name, s, arriving=False):
        slot = ready(name)
        n = rowb.shape[2]

        def step(i, total):
            tiles = [far_first(NT - 1 - (i * GROUP + g)) for g in range(GROUP)]
            if arriving:
                for t in tiles:
                    take(rowb.at[s, t], sbr.at[s, t])
            for t in tiles:
                left = stacked(rowb[s, t])
                high, low = split_rows(wbuf[slot, pl.ds(pl.multiple_of(t * CH, CH), CH), :])
                total += jnp.dot(left, high, preferred_element_type=jnp.float32)
                total += jnp.dot(left, low, preferred_element_type=jnp.float32)
            return total

        total = lax.fori_loop(0, NT // GROUP, step, jnp.zeros((2 * n, W), jnp.float32))
        used(name)
        return total[:n] + total[n:]

    @pl.when(diag)
    def _():
        for q in range(nred):
            gat[0, q] = rhs_ref[0, :, pl.ds(pl.multiple_of(part * W + q * CH, CH), CH)]
        for d in range(1, R):
            remote(gat.at[0], gat.at[0], s2s.at[0], s2r.at[0, 0], lax.rem(r + d, R), c).start()

    def end_first():
        @pl.when(diag)
        def _():
            take(xr.at[pl.ds(0, R - 1)], s2s.at[0])
    ends.append(end_first)
    own = c == r * ratio
    for k in range(1, count):
        for t in range(NT):
            pend[k, t] = jnp.where(own, rhs_ref[k, :, t * CH:(t + 1) * CH], 0.0)

    prefetch(2)

    @pl.when(jnp.logical_not(diag))
    def _():
        take(gat.at[0], s2r.at[0, 0])

    late = []

    def fill_late():
        if late:
            i, k, s = late.pop(0)

            def emit(t, value, i=i):
                pend[i, t] = pend[i, t] - value
            times_rows(L(i, k), s, emit)

    col_at = 0
    stage = 0
    for k in range(count):
        def emit(t, value, s=stage):
            send1[s, t] = value
            scatter_tile(s, t)
        (times_rows if k == 0 else times_rows_arriving)(M(k), col_at, emit)
        scatter_rows_ends(stage)
        prefetch(2)
        fill_late()
        entry = stage + 1
        sum_rows(stage, entry)
        stage += 1
        if k == count - 1:
            break
        gather_start(gat.at[entry], s2s.at[entry], s2r.at[entry, r])
        late = late + [(i, k, entry) for i in range(k + 2, count)]

        def emit_l(t, value, s=stage, i=k + 1):
            send1[s, t] = pend[i, t] - value
            scatter_tile(s, t)
        times_rows_arriving(L(k + 1, k), entry, emit_l)
        scatter_rows_ends(stage)
        prefetch(2)
        late.sort(key=lambda n: n[0])
        fill_late()
        entry = stage + 1
        sum_rows(stage, entry)
        gather_start(gat.at[entry], s2s.at[entry], s2r.at[entry, r])
        col_at = entry
        stage += 1

    def pivot(k):
        return piv_ref[k:k + 1, pl.ds(pl.multiple_of(c * W + r * CH, CH), CH)]

    n_cols = 0
    n_rows = 0

    def scale_last():
        wb[count - 1] = gat[2 * count - 1, r] / pivot(count - 1)
    reducers(scale_last)
    spread_rows(0, wb.at[count - 1])
    n_rows = 1
    blate = []

    def fill_blate():
        if blate:
            i, j, s = blate.pop(0)
            total = times_cols(L(i, j), s)
            if i == count - 1:
                bpend[j] = total
            else:
                bpend[j] = bpend[j] + total

    def put_cols(total, s):
        for q in range(nred):
            senda[s, q] = total[:, q * CH:(q + 1) * CH]

    for k in reversed(range(count)):
        prefetch(2)
        fill_blate()
        total = times_cols(M(k), n_rows - 1, True)
        if k == 0:
            for q in range(nred):
                xs[q] = total[:, q * CH:(q + 1) * CH]
            for d in range(1, R):
                remote(xs, xr.at[r], sfs.at[0], sfr.at[0], lax.rem(r + d, R), c).start()
            xr[r] = xs[...]
            break
        put_cols(total, n_cols)
        scatter_cols(n_cols)
        prefetch(2)

        def keep_answer(k=k, s=n_cols):
            xg[k, r] = sum_cols(s)
        reducers(keep_answer)
        n_cols += 1
        spread_rows(n_rows, xg.at[k, r])
        n_rows += 1
        gather_start(xg.at[k], sxs.at[k], sxr.at[k])
        fill_blate()
        total = times_cols(L(k, k - 1), n_rows - 1, True)
        if k < count - 1:
            total = bpend[k - 1] + total
        put_cols(total, n_cols)
        scatter_cols(n_cols)
        prefetch(2)

        def scale(k=k, s=n_cols):
            wb[k - 1] = gat[2 * k - 1, r] / pivot(k - 1) - sum_cols(s)
        reducers(scale)
        n_cols += 1
        spread_rows(n_rows, wb.at[k - 1])
        n_rows += 1
        blate = blate + [(k, j, n_rows - 2) for j in reversed(range(k - 1))]
        blate.sort(key=lambda n: -n[1])

    for k in range(1, count):
        gather_wait(xg.at[k], sxr.at[k])
        for q in range(nred):
            out_ref[k, :, q * CH:(q + 1) * CH] = xg[k, q]
    for end in ends:
        end()
    take(xr.at[pl.ds(0, R - 1)], sfr.at[0])
    summed = jnp.sum(xr[...], axis=0)
    for q in range(nred):
        out_ref[0, :, q * CH:(q + 1) * CH] = summed[q]
    take(xr.at[pl.ds(0, R - 1)], sfs.at[0])
    assert position[0] == len(uses)


def local(R, C, rhs, off_blocks, inverse_blocks, pivots):
    count, rows_tile, W = inverse_blocks.shape
    n = rhs.shape[1]
    nred = max(1, min(R, W // 128))
    CH = W // nred
    NT = rows_tile // CH
    f32 = jnp.float32
    blocks = count + off_blocks.shape[0]
    slots = min(blocks, (56 << 20) // (rows_tile * W * 4))
    dma = pltpu.SemaphoreType.DMA
    vmem = pl.BlockSpec(memory_space=pltpu.VMEM)
    hbm = pl.BlockSpec(memory_space=pl.ANY)
    return pl.pallas_call(
        functools.partial(kernel, R, C),
        out_shape=jax.ShapeDtypeStruct((count, n, W), f32),
        in_specs=[vmem, vmem, hbm, hbm],
        out_specs=vmem,
        scratch_shapes=[
            pltpu.VMEM((slots, rows_tile, W), f32),
            pltpu.VMEM((NT, n, CH), f32),
            pltpu.VMEM((count, NT, n, CH), f32),
            pltpu.VMEM((count, n, W), f32),
            pltpu.VMEM((count, n, CH), f32),
            pltpu.VMEM((2 * count - 1, NT, n, CH), f32),
            pltpu.VMEM((2 * count - 1, C, n, CH), f32),
            pltpu.VMEM((2 * count, nred, n, CH), f32),
            pltpu.VMEM((2 * count - 2, nred, n, CH), f32),
            pltpu.VMEM((2 * count - 2, R, n, CH), f32),
            pltpu.VMEM((2 * count - 1, NT, n, CH), f32),
            pltpu.VMEM((count, nred, n, CH), f32),
            pltpu.VMEM((nred, n, CH), f32),
            pltpu.VMEM((R, nred, n, CH), f32),
            dma((2 * blocks,)),
            dma((2 * count - 1,)), dma((2 * count - 1,)),
            dma((2 * count,)), dma((2 * count, R)),
            dma((2 * count - 2,)), dma((2 * count - 2,)),
            dma((2 * count - 1,)), dma((2 * count - 1, NT)),
            dma((count,)), dma((count,)),
            dma((1,)), dma((1,)),
        ],
        compiler_params=pltpu.CompilerParams(
            collective_id=0, has_side_effects=True, vmem_limit_bytes=67043328),
    )(rhs, pivots, off_blocks, inverse_blocks)


def solution(mesh):
    return jax.shard_map(
        functools.partial(local, mesh.shape["row"], mesh.shape["col"]),
        mesh=mesh,
        in_specs=(P(None, None, "row"), P(None, "row", "col"), P(None, "row", "col"), P()),
        out_specs=P(None, None, "col"),
        check_vma=False,
    )
```
